32 devices in a mesh: ctx: 16 (over z, x, core), tp: 2 (over y).
Axes of the slice: x: 2, y: 2, z: 4, core: 2. Of those that a mesh axis runs over, the one named last changes fastest.
Arguments:
- doc_lengths: int32 [32], replicated, may hold values from 1 to 512, 2048 in all
- ssm_x: bfloat16 [2048, 8192], P('ctx', 'tp'), may hold values from -6 to 6
- ssm_gate: bfloat16 [2048, 8192], P('ctx', 'tp'), may hold values from -6 to 6
- ssm_b: bfloat16 [2048, 2048], P('ctx', 'tp'), may hold values from -6 to 6
- ssm_c: bfloat16 [2048, 2048], P('ctx', 'tp'), may hold values from -0.375 to 0.375
- step_size: float32 [2048, 128], P('ctx', 'tp'), as said below
- decay_rate: float32 [128], P('tp'), as said below
- norm_weight: float32 [8192], P('tp'), may hold values from 0.1 to 1.9
- queries: bfloat16 [2048, 8192], P('ctx', 'tp'), may hold values from -96 to 96
- keys: bfloat16 [2048, 1024], P('ctx', 'tp'), may hold values from -4 to 4
- values: bfloat16 [2048, 1024], P('ctx', 'tp'), may hold values from -6 to 6
Outputs:
- mixed: bfloat16 [2048, 8192], P(('ctx', 'tp'))
- attended: bfloat16 [2048, 8192], P(('ctx', 'tp'))
The draws below stay inside these ranges and needn't reach their ends.
Inputs may be any that keep to these rules, and one draw needn't show every extreme that they name: `doc_lengths`: every document has at least one token; the longest has exactly 512. `step_size`: Positive. `decay_rate`: Positive, at most 0.04.
All inputs are finite; a program needn't handle non-finite values.
Results may differ from the reference program's by a relative error of at most 0.0049.
Values may be sent and summed in bfloat16 or wider, within the bound.
A program may use at most 192 MiB of HBM per device.

```python
import math
import jax
import jax.numpy as jnp
import numpy as np
from jax import lax

HEADS = 128
HEAD_DIM = 64
STATE = 256
GROUPS = 8
QHEADS = 64
KVHEADS = 8
ATT_DIM = 128
TOK_DEV = 128
NDOC = 32
SEQ = 2048
MAXDOC = 512


def log_uniform(key, out_shape, low_end, high_end):
    unit_draw = jax.random.uniform(key, out_shape, jnp.float32)
    return jnp.exp(math.log(low_end) + unit_draw * math.log(high_end / low_end))


def draw_decay_rate(key, part):
    head_order = jax.random.permutation(jax.random.fold_in(key, 11), HEADS)
    slow_rate = log_uniform(jax.random.fold_in(key, 12), (HEADS,), 0.3, 1.0) / MAXDOC
    fast_rate = log_uniform(jax.random.fold_in(key, 13), (HEADS,), 0.02, 0.04)
    fast_count = HEADS // 2
    return jnp.where(head_order < fast_count, fast_rate, slow_rate).astype(jnp.float32)


def draw_step_size(key, part):
    block_count = SEQ // TOK_DEV
    coarse = log_uniform(jax.random.fold_in(key, 21), (block_count, HEADS), 0.5, 2.0)
    fine_part = log_uniform(jax.random.fold_in(key, 22), (SEQ, HEADS), 0.5, 2.0)
    return (jnp.repeat(coarse, TOK_DEV, axis=0) * fine_part).astype(jnp.float32)


def attention_pair(key):
    base_key = jax.random.fold_in(key, 31)
    q_groups = QHEADS // KVHEADS
    keys_f = jnp.clip(jax.random.normal(jax.random.fold_in(base_key, 1), (SEQ, KVHEADS, ATT_DIM), jnp.float32), -4.0, 4.0)
    queries_f = jnp.clip(jax.random.normal(jax.random.fold_in(base_key, 2), (SEQ, KVHEADS, q_groups, ATT_DIM), jnp.float32), -4.0, 4.0)
    return (queries_f.reshape(SEQ, QHEADS * ATT_DIM), keys_f.reshape(SEQ, KVHEADS * ATT_DIM))


def draw_queries(key, part):
    return attention_pair(key)[0].astype(jnp.bfloat16)


def draw_keys(key, part):
    return attention_pair(key)[1].astype(jnp.bfloat16)


def shard_levels(own_key, extent, cuts, smallest, largest):
    def one(position, blocks):
        steps = jax.random.uniform(jax.random.fold_in(jax.random.fold_in(own_key, 6), position), (blocks,), jnp.float32, smallest / len(cuts), largest / len(cuts))
        return jnp.repeat(jnp.exp(steps), extent[position] // blocks).reshape((-1,) + (1,) * (len(extent) - position - 1))

    factor_of = one(*cuts[0])
    for cut in cuts[1:]:
        factor_of = factor_of * one(*cut)
    return factor_of


def profile(number_of, total, reach, lean):
    loads = [(1 << 20) // math.isqrt(rank ** lean) + 1 for rank in range(2, number_of + 1)]
    spare, holding = total - reach - (number_of - 1), [1] * (number_of - 1)
    while spare > 0:
        candidates = [i for i in range(number_of - 1) if holding[i] < reach]
        whole, remaining = sum([loads[i] for i in candidates]), spare
        for i in candidates:
            addition = min(reach - holding[i], max(1, remaining * loads[i] // whole), spare)
            holding[i] = holding[i] + addition
            spare = spare - addition
    return np.array([reach] + holding)


def ragged(stream_key, count, total, bound, lean):
    if count == 2:
        one = jax.random.randint(stream_key, (), max(1, total - bound), min(bound, total - 1) + 1)
        return jnp.stack([one, total - one])
    sizes = jnp.asarray(profile(count, total, bound, lean), jnp.int32)
    pairs = (count - 1) // 2
    donor, taker = sizes[1:1 + 2 * pairs:2], sizes[2:2 + 2 * pairs:2]
    slack = jnp.minimum(donor - 1, bound - taker)
    passed = jax.random.randint(jax.random.fold_in(stream_key, 1), (pairs,), 0, 1 << 20) % (slack + 1)
    sizes = sizes.at[1:1 + 2 * pairs:2].set(donor - passed).at[2:2 + 2 * pairs:2].set(taker + passed)
    return sizes[jax.random.permutation(jax.random.fold_in(stream_key, 2), count)]


def normal_values(stream_key, extent, scale, most, pieces=(), held_as=jnp.bfloat16):
    drawn = scale * jax.random.normal(stream_key, extent, jnp.float32)
    if pieces:
        drawn = drawn * shard_levels(stream_key, extent, pieces, -0.22, 0.18)
    return jnp.clip(drawn, -most, most).astype(held_as)


def setup_inputs(seed: int = 0) -> dict:
    streams_of = jax.random.split(jax.random.key(seed), 12)
    return {
        "doc_lengths": ragged(streams_of[0], NDOC, SEQ, MAXDOC, 2).astype(jnp.int32),
        "ssm_x": normal_values(streams_of[1], (SEQ, HEADS * HEAD_DIM), 1.0, 6.0, ((0, 16), (1, 2))),
        "ssm_gate": normal_values(streams_of[2], (SEQ, HEADS * HEAD_DIM), 1.0, 6.0, ((0, 16), (1, 2))),
        "ssm_b": normal_values(streams_of[3], (SEQ, GROUPS * STATE), 1.0, 6.0, ((0, 16), (1, 2))),
        "ssm_c": normal_values(streams_of[4], (SEQ, GROUPS * STATE), STATE ** -0.5, 0.375, ((0, 16), (1, 2))),
        "step_size": draw_step_size(jax.random.fold_in(streams_of[11], 71), 0),
        "decay_rate": draw_decay_rate(jax.random.fold_in(streams_of[11], 71), 0),
        "norm_weight": jnp.clip(1.0 + 0.18 * jax.random.normal(streams_of[7], (HEADS * HEAD_DIM,), jnp.float32), 0.1, 1.9),
        "queries": draw_queries(jax.random.fold_in(streams_of[11], 71), 0),
        "keys": draw_keys(jax.random.fold_in(streams_of[11], 71), 0),
        "values": normal_values(streams_of[10], (SEQ, KVHEADS * ATT_DIM), 1.0, 6.0, ((0, 16), (1, 2))),
    }


def doc_starts(doc_lengths):
    return (jnp.cumsum(doc_lengths) - doc_lengths).astype(jnp.int32)

def doc_index(positions, starts):
    return (lax.optimization_barrier(jnp.sum((starts[None, :] <= positions[:, None]).astype(jnp.int32), axis=1)) - 1).astype(jnp.int32)

def block_terms(ssm_x, ssm_b, ssm_c, step_size, decay_rate, doc_ids, prev_id, group_heads):
    tok_rows = ssm_x.shape[0]
    head_count = step_size.shape[1]
    group_count = head_count // group_heads
    head_size = ssm_x.shape[1] // head_count
    state_size = ssm_b.shape[1] // group_count
    inputs = ssm_x.reshape(tok_rows, group_count, group_heads, head_size)
    in_proj = ssm_b.reshape(tok_rows, group_count, state_size)
    out_proj = ssm_c.reshape(tok_rows, group_count, state_size)
    log_decay = -(step_size * decay_rate[None, :])
    cumulative = jnp.cumsum(log_decay, axis=0)
    same_doc = doc_ids[:, None] == doc_ids[None, :]
    causal = jnp.arange(tok_rows)[:, None] >= jnp.arange(tok_rows)[None, :]
    allowed = (same_doc & causal)[None]
    spread = cumulative.T[:, :, None] - cumulative.T[:, None, :]
    weights = jnp.where(allowed, jnp.exp(jnp.where(allowed, spread, 0.0)), 0.0) * step_size.T[:, None, :]
    intersection = jnp.einsum('tgn,sgn->gts', out_proj.astype(jnp.float32), in_proj.astype(jnp.float32))
    mixing = (weights.reshape(group_count, group_heads, tok_rows, tok_rows) * intersection[:, None]).astype(jnp.bfloat16)
    y_intra = jnp.einsum('ghts,sghp->tghp', mixing.astype(jnp.float32), inputs.astype(jnp.float32))
    final_sum = cumulative[-1]
    tail = jnp.exp(final_sum[None, :] - cumulative) * step_size * (doc_ids == doc_ids[-1]).astype(jnp.float32)[:, None]
    scaled = (inputs.astype(jnp.float32) * tail.reshape(tok_rows, group_count, group_heads)[..., None]).astype(jnp.bfloat16)
    state_local = jnp.einsum('sghp,sgn->ghpn', scaled.astype(jnp.float32), in_proj.astype(jnp.float32))
    entry = jnp.exp(cumulative) * (doc_ids == prev_id).astype(jnp.float32)[:, None]
    transmit = jnp.exp(final_sum) * (doc_ids[-1] == prev_id).astype(jnp.float32)
    return (y_intra, state_local, entry, transmit.reshape(group_count, group_heads))

def finish_rows(y_intra, entry, carried, ssm_c, ssm_gate, norm_weight):
    tok_rows, group_count, group_heads, head_size = y_intra.shape
    out_proj = ssm_c.reshape(tok_rows, group_count, -1).astype(jnp.float32)
    incoming = jnp.einsum('tgn,ghpn->tghp', out_proj, carried, precision=lax.Precision.HIGHEST)
    mixer_out = y_intra + incoming * entry.reshape(tok_rows, group_count, group_heads)[..., None]
    gate_vals = ssm_gate.reshape(tok_rows, group_count, group_heads, head_size).astype(jnp.float32)
    gated = (mixer_out * jax.nn.silu(gate_vals)).reshape(tok_rows, group_count, group_heads * head_size)
    factor = lax.rsqrt(lax.optimization_barrier(jnp.mean(gated * gated, axis=2, keepdims=True)) + 1e-05)
    return ((gated * factor).reshape(tok_rows, -1) * norm_weight[None, :]).astype(jnp.bfloat16)

def take_rows(array, begin, count):
    return lax.dynamic_slice_in_dim(array, begin, count, 0)

def reference(doc_lengths, ssm_x, ssm_gate, ssm_b, ssm_c, step_size, decay_rate, norm_weight, queries, keys, values):
    starts = doc_starts(doc_lengths)
    block_count = SEQ // TOK_DEV
    group_heads = HEADS // GROUPS

    def mixer_block(carried, block_index):
        begin = (block_index * TOK_DEV).astype(jnp.int32)
        positions = begin + jnp.arange(TOK_DEV, dtype=jnp.int32)
        doc_ids = doc_index(positions, starts)
        prev_id = doc_index(jnp.reshape(begin - 1, (1,)).astype(jnp.int32), starts)[0]
        y_intra, state_local, entry, transmit = block_terms(take_rows(ssm_x, begin, TOK_DEV), take_rows(ssm_b, begin, TOK_DEV), take_rows(ssm_c, begin, TOK_DEV), take_rows(step_size, begin, TOK_DEV), decay_rate, doc_ids, prev_id, group_heads)
        rows_out = finish_rows(y_intra, entry, carried, take_rows(ssm_c, begin, TOK_DEV), take_rows(ssm_gate, begin, TOK_DEV), norm_weight)
        return (transmit[:, :, None, None] * carried + state_local, rows_out)
    start_state = jnp.zeros((GROUPS, group_heads, HEAD_DIM, STATE), jnp.float32)
    unused_state, mixed_blocks = lax.scan(mixer_block, start_state, jnp.arange(block_count, dtype=jnp.int32))
    mixed = mixed_blocks.reshape(SEQ, HEADS * HEAD_DIM)
    q_groups = QHEADS // KVHEADS
    window = MAXDOC + TOK_DEV
    scale = ATT_DIM ** (-0.5)

    def attention_block(block_index):
        begin = (block_index * TOK_DEV).astype(jnp.int32)
        window_begin = jnp.maximum(begin - MAXDOC, 0).astype(jnp.int32)
        query_rows = take_rows(queries, begin, TOK_DEV).reshape(TOK_DEV, KVHEADS, q_groups, ATT_DIM).astype(jnp.float32)
        key_rows = take_rows(keys, window_begin, window).reshape(window, KVHEADS, ATT_DIM).astype(jnp.float32)
        value_rows = take_rows(values, window_begin, window).reshape(window, KVHEADS, ATT_DIM).astype(jnp.float32)
        query_pos = begin + jnp.arange(TOK_DEV, dtype=jnp.int32)
        key_pos = window_begin + jnp.arange(window, dtype=jnp.int32)
        allowed = (doc_index(query_pos, starts)[:, None] == doc_index(key_pos, starts)[None, :]) & (key_pos[None, :] <= query_pos[:, None])
        scores = jnp.einsum('tngd,knd->ngtk', query_rows, key_rows) * scale
        scores = jnp.where(allowed[None, None], scores, -jnp.inf)
        top_score = lax.optimization_barrier(jnp.max(scores, axis=3, keepdims=True))
        probs = jnp.exp(scores - top_score)
        total = lax.optimization_barrier(jnp.sum(probs, axis=3))
        rounded = lax.optimization_barrier(probs.astype(jnp.bfloat16))
        summed = jnp.einsum('ngtk,knd->ngtd', rounded.astype(jnp.float32), value_rows)
        result = summed / total[..., None]
        return jnp.transpose(result, (2, 0, 1, 3)).reshape(TOK_DEV, -1).astype(jnp.bfloat16)
    attended = lax.map(attention_block, jnp.arange(block_count, dtype=jnp.int32)).reshape(SEQ, QHEADS * ATT_DIM)
    return (mixed, attended)
```

```python
import jax
import jax.numpy as jnp
from jax import lax
from jax.experimental import pallas as pl
from jax.experimental.pallas import tpu as pltpu
from jax.sharding import PartitionSpec as P

HEADS = 128
GROUPS = 8
ATT_DIM = 128
DOC_DEVS = 4


NEG_LARGE = -1e30


def for_sending(x):
    return jax.tree.map(lambda a: a.astype(jnp.bfloat16) if a.dtype == jnp.float32 else a, x)


def passed_along(block, axis, distance):
    devices = range(lax.axis_size(axis))
    route = [(i - distance, i) for i in devices if i - distance in devices]
    return lax.ppermute(block, axis, route)


def doc_starts(doc_lengths):
    return jnp.cumsum(doc_lengths) - doc_lengths


def doc_index(positions, starts):
    return jnp.sum((starts[None, :] <= positions[:, None]).astype(jnp.int32), axis=1) - 1


def block_terms(ssm_x, ssm_b, ssm_c, step_size, decay_rate, doc_ids, prev_id, group_heads):
    tok_rows = ssm_x.shape[0]
    head_count = step_size.shape[1]
    group_count = head_count // group_heads
    head_size = ssm_x.shape[1] // head_count
    state_size = ssm_b.shape[1] // group_count
    inputs = ssm_x.reshape(tok_rows, group_count, group_heads, head_size)
    in_proj = ssm_b.reshape(tok_rows, group_count, state_size)
    out_proj = ssm_c.reshape(tok_rows, group_count, state_size)
    log_decay = -(step_size * decay_rate[None, :])
    cumulative = jnp.cumsum(log_decay, axis=0)
    same_doc = doc_ids[:, None] == doc_ids[None, :]
    causal = jnp.arange(tok_rows)[:, None] >= jnp.arange(tok_rows)[None, :]
    allowed = (same_doc & causal)[None]
    spread = cumulative.T[:, :, None] - cumulative.T[:, None, :]
    weights = (
        jnp.where(allowed, jnp.exp(jnp.where(allowed, spread, 0.0)), 0.0) * step_size.T[:, None, :]
    )
    intersection = jnp.einsum("tgn,sgn->gts", out_proj, in_proj, preferred_element_type=jnp.float32)
    mixing = (
        weights.reshape(group_count, group_heads, tok_rows, tok_rows) * intersection[:, None]
    ).astype(jnp.bfloat16)
    y_intra = jnp.einsum("ghts,sghp->tghp", mixing, inputs, preferred_element_type=jnp.float32)
    final_sum = cumulative[-1]
    tail = (
        jnp.exp(final_sum[None, :] - cumulative)
        * step_size
        * (doc_ids == doc_ids[-1]).astype(jnp.float32)[:, None]
    )
    scaled = (
        inputs.astype(jnp.float32) * tail.reshape(tok_rows, group_count, group_heads)[..., None]
    ).astype(jnp.bfloat16)
    state_local = jnp.einsum("sghp,sgn->ghpn", scaled, in_proj, preferred_element_type=jnp.float32)
    entry = jnp.exp(cumulative) * (doc_ids == prev_id).astype(jnp.float32)[:, None]
    transmit = jnp.exp(final_sum) * (doc_ids[-1] == prev_id).astype(jnp.float32)
    return (y_intra, state_local, entry, transmit.reshape(group_count, group_heads))


def finish_rows(y_intra, entry, carried, ssm_c, ssm_gate, norm_weight):
    tok_rows, group_count, group_heads, head_size = y_intra.shape
    out_proj = ssm_c.reshape(tok_rows, group_count, -1).astype(jnp.float32)
    incoming = jnp.einsum("tgn,ghpn->tghp", out_proj, carried, precision=lax.Precision.HIGHEST)
    mixer_out = y_intra + incoming * entry.reshape(tok_rows, group_count, group_heads)[..., None]
    gate_vals = ssm_gate.reshape(tok_rows, group_count, group_heads, head_size).astype(jnp.float32)
    gated = (mixer_out * jax.nn.silu(gate_vals)).reshape(
        tok_rows, group_count, group_heads * head_size
    )
    factor = lax.rsqrt(jnp.mean(gated * gated, axis=2, keepdims=True) + 1e-05)
    return ((gated * factor).reshape(tok_rows, -1) * norm_weight[None, :]).astype(jnp.bfloat16)


def chain_states(earlier, later):
    return (earlier[0] * later[0], later[0][:, :, None, None] * earlier[1] + later[1])


def attention_update(
    carry, query_rows, key_block, value_block, key_pos, query_pos, query_doc, starts
):
    running_max, running_sum, running_acc = carry
    block_rows = key_block.shape[0]
    kv_local = key_block.shape[1] // ATT_DIM
    key_heads = key_block.reshape(block_rows, kv_local, ATT_DIM)
    value_heads = value_block.reshape(block_rows, kv_local, ATT_DIM)
    key_doc = doc_index(key_pos, starts)
    allowed = (query_doc[:, None] == key_doc[None, :]) & (key_pos[None, :] <= query_pos[:, None])
    scores = jnp.einsum(
        "tngd,knd->ngtk", query_rows, key_heads, preferred_element_type=jnp.float32
    ) * ATT_DIM ** (-0.5)
    scores = jnp.where(allowed[None, None], scores, -jnp.inf)
    new_max = jnp.maximum(running_max, jnp.max(scores, axis=3))
    probs = jnp.exp(scores - new_max[..., None])
    factor = jnp.exp(running_max - new_max)
    new_sum = running_sum * factor + jnp.sum(probs, axis=3)
    weighted = jnp.einsum(
        "ngtk,knd->ngtd",
        probs.astype(jnp.bfloat16),
        value_heads,
        preferred_element_type=jnp.float32,
    )
    return (new_max, new_sum, running_acc * factor[..., None] + weighted)


def local_any(
    doc_lengths,
    ssm_x,
    ssm_gate,
    ssm_b,
    ssm_c,
    step_size,
    decay_rate,
    norm_weight,
    queries,
    keys,
    values,
):
    tok_rows = ssm_x.shape[0]
    ctx_index = lax.axis_index("ctx")
    begin = ctx_index * tok_rows
    positions = begin + jnp.arange(tok_rows, dtype=jnp.int32)
    starts = doc_starts(doc_lengths)
    doc_ids = doc_index(positions, starts)
    prev_id = doc_index(jnp.reshape(begin - 1, (1,)), starts)[0]
    group_heads = HEADS // GROUPS
    y_intra, state_local, entry, transmit = block_terms(
        ssm_x, ssm_b, ssm_c, step_size, decay_rate, doc_ids, prev_id, group_heads
    )
    merged = (transmit, state_local)
    for level_bit in range(DOC_DEVS.bit_length() - 1):
        earlier = passed_along(
            (for_sending(merged[0]), for_sending(merged[1])), "ctx", 1 << level_bit
        )
        merged = chain_states(earlier, merged)
    carried = passed_along(merged[1], "ctx", 1)
    mixed_rows = finish_rows(y_intra, entry, carried, ssm_c, ssm_gate, norm_weight)
    kv_local = keys.shape[1] // ATT_DIM
    q_groups = queries.shape[1] // (kv_local * ATT_DIM)
    query_rows = queries.reshape(tok_rows, kv_local, q_groups, ATT_DIM)
    floor_start = jnp.max(jnp.where(starts <= begin, starts, 0))
    query_last = begin + tok_rows - 1
    carry_shape = (kv_local, q_groups, tok_rows)
    initial = (
        jnp.full(carry_shape, NEG_LARGE, jnp.float32),
        jnp.zeros(carry_shape, jnp.float32),
        jnp.zeros(carry_shape + (ATT_DIM,), jnp.float32),
    )

    def visit(carry, key_block, value_block, key_begin):
        block_rows = key_block.shape[0]
        needed = (key_begin <= query_last) & (key_begin + block_rows - 1 >= floor_start)

        def update(inner):
            key_pos = key_begin + jnp.arange(block_rows, dtype=jnp.int32)
            return attention_update(
                inner, query_rows, key_block, value_block, key_pos, positions, doc_ids, starts
            )

        def unchanged(inner):
            return inner

        return lax.cond(needed, update, unchanged, carry)

    totals = visit(initial, keys, values, begin)
    for hop_count in range(1, DOC_DEVS + 1):
        near_keys, near_values = passed_along((keys, values), "ctx", hop_count)
        totals = visit(totals, near_keys, near_values, begin - hop_count * tok_rows)
    final_out = totals[2] / totals[1][..., None]
    attended_rows = (
        jnp.transpose(final_out, (2, 0, 1, 3)).reshape(tok_rows, -1).astype(jnp.bfloat16)
    )
    mixed_local, attended_local = (
        lax.all_to_all(mixed_rows, "tp", split_axis=0, concat_axis=1, tiled=True),
        lax.all_to_all(attended_rows, "tp", split_axis=0, concat_axis=1, tiled=True),
    )
    return (mixed_local, attended_local)


LOG2E = 1.4426950408889634
F32 = jnp.float32
BF16 = jnp.bfloat16


def dot(a, b, dims=(((1,), (0,)), ((), ()))):
    return lax.dot_general(a, b, dims, preferred_element_type=F32)


def stacked(first, own, received):
    return jnp.where(first, own, received), jnp.where(first, received, own)


def spread_heads(columns, tile, lanes, head_size):
    per = lanes // head_size
    lane = lax.broadcasted_iota(jnp.int32, (columns.shape[0], lanes), 1)
    wide = jnp.broadcast_to(columns[:, tile * per : tile * per + 1], lane.shape)
    for k in range(1, per):
        column = columns[:, tile * per + k : tile * per + k + 1]
        wide = jnp.where(lane >= k * head_size, column, wide)
    return wide


def state_kernel(x_ref, b_ref, tail_ref, s_ref, scaled):
    heads = tail_ref.shape[2]
    width = x_ref.shape[1]
    tail = tail_ref[0]
    for tile in range(width // 128):
        cols = slice(tile * 128, tile * 128 + 128)
        wide = spread_heads(tail, tile, 128, width // heads)
        scaled[:, cols] = (x_ref[:, cols].astype(F32) * wide).astype(BF16)
    s_ref[...] = dot(b_ref[...], scaled[...], (((0,), (0,)), ((), ()))).astype(BF16)


def intra_kernel(x_ref, b_ref, c_ref, l_ref, lt_ref, dtt_ref, dq_ref, dk_ref, y_ref):
    rows, width = x_ref.shape
    heads = l_ref.shape[2]
    head_size = width // heads
    at = lax.broadcasted_iota(jnp.int32, (rows, rows), 0)
    to = lax.broadcasted_iota(jnp.int32, (rows, rows), 1)
    bias = jnp.where((dq_ref[...] == dk_ref[...]) & (to <= at), 0.0, NEG_LARGE)
    inter = dot(c_ref[...], b_ref[...], (((1,), (1,)), ((), ())))
    lcol, lrow, step = l_ref[0], lt_ref[0], dtt_ref[0]
    per = 128 // head_size
    lane = lax.broadcasted_iota(jnp.int32, (rows, 128), 1)
    for tile in range(width // 128):
        cols = slice(tile * 128, tile * 128 + 128)
        total = None
        for k in range(per):
            h = tile * per + k
            w = jnp.exp((lcol[:, h : h + 1] - lrow[h : h + 1, :]) + bias)
            mix = (w * step[h : h + 1, :] * inter).astype(BF16)
            part = dot(mix, x_ref[:, cols])
            total = part if k == 0 else jnp.where(lane >= k * head_size, part, total)
        y_ref[:, cols] = total


def finish_kernel(y_ref, c_ref, s1_ref, s2_ref, t_ref, entry_ref, gate_ref, w_ref, o_ref, gated):
    rows, width = y_ref.shape
    heads = entry_ref.shape[2]
    entry = entry_ref[0]
    carried = (
        s1_ref[...].astype(F32) + t_ref[...] * s2_ref[...].astype(F32)
    ).astype(BF16)
    gated[...] = dot(c_ref[...], carried)
    square = jnp.zeros((rows, 128), F32)
    for tile in range(width // 128):
        cols = slice(tile * 128, tile * 128 + 128)
        wide = spread_heads(entry, tile, 128, width // heads)
        z = gate_ref[:, cols].astype(F32)
        out = (y_ref[:, cols] + gated[:, cols] * wide) * (z / (1.0 + jnp.exp(-z)))
        gated[:, cols] = out
        square += out * out
    mean = jnp.sum(square, axis=1, keepdims=True) * (1.0 / width)
    factor = lax.rsqrt(mean + 1e-05)
    o_ref[...] = (gated[...] * factor * w_ref[...]).astype(BF16)


def attention_kernel(q_ref, k2_ref, v2_ref, k1_ref, v1_ref, k0_ref, v0_ref, dq_ref, dk_ref, o_ref):
    rows, width = q_ref.shape
    total_keys = 3 * rows
    keys = jnp.concatenate([k2_ref[...], k1_ref[...], k0_ref[...]], axis=0)
    vals = jnp.concatenate([v2_ref[...], v1_ref[...], v0_ref[...]], axis=0)
    at = lax.broadcasted_iota(jnp.int32, (rows, total_keys), 0) + 2 * rows
    to = lax.broadcasted_iota(jnp.int32, (rows, total_keys), 1)
    bias = jnp.where((dq_ref[...] == dk_ref[...]) & (to <= at), 0.0, NEG_LARGE)
    scale = LOG2E * ATT_DIM ** (-0.5)
    for head in range(width // ATT_DIM):
        cols = slice(head * ATT_DIM, (head + 1) * ATT_DIM)
        scores = dot(q_ref[:, cols], keys, (((1,), (1,)), ((), ()))) + bias
        top = jnp.max(scores, axis=1, keepdims=True)
        probs = jnp.exp2((scores - top) * scale)
        total = jnp.sum(probs, axis=1, keepdims=True)
        o_ref[:, cols] = (dot(probs.astype(BF16), vals) / total).astype(BF16)


def local_pair(
    doc_lengths,
    ssm_x,
    ssm_gate,
    ssm_b,
    ssm_c,
    step_size,
    decay_rate,
    norm_weight,
    queries,
    keys,
    values,
):
    n = lax.axis_size("ctx")
    index = lax.axis_index("ctx")
    tp_index = lax.axis_index("tp")
    parity, pair = index % 2, index // 2
    first = parity == 0
    tok = ssm_x.shape[0]
    rows = 2 * tok
    group_heads = HEADS // GROUPS
    groups = step_size.shape[1] // group_heads // 2
    heads = groups * group_heads

    def half(array, which, axis=1):
        size = array.shape[axis] // 2
        return lax.dynamic_slice_in_dim(array, which * size, size, axis)

    def both(array):
        received = lax.ppermute(half(array, 1 - parity), "ctx", [(j, j ^ 1) for j in range(n)])
        own = half(array, parity)
        return jnp.concatenate(stacked(first, own, received), axis=0)

    def skipped(array):
        return lax.ppermute(array, "ctx", [(j, j + 4) for j in range(n - 4)])

    def crossed(array, far):
        odd = pair % 2 == 1
        route = [(j, j + 2) if (j // 2) % 2 == 0 else (j, j - 2) for j in range(n)]
        return lax.ppermute(jnp.where(odd, far, array), "ctx", route)

    x = both(ssm_x)
    b = both(ssm_b)
    step = both(step_size)
    kv_width = keys.shape[1] // 2
    own_kv = jnp.concatenate([half(keys, 1 - parity), half(values, 1 - parity)], axis=1)
    got_kv = lax.ppermute(own_kv, "ctx", [(j, j ^ 1) for j in range(n)])
    kept_kv = jnp.concatenate([half(keys, parity), half(values, parity)], axis=1)
    kv = jnp.concatenate(stacked(first, kept_kv, got_kv), axis=0)
    q = both(queries)
    c = both(ssm_c)
    gate = both(ssm_gate)

    starts = doc_starts(doc_lengths)
    begin = pair * rows
    positions = begin - 2 * rows + jnp.arange(3 * rows, dtype=jnp.int32)
    all_docs = doc_index(positions, starts)
    doc_ids = all_docs[2 * rows :]
    prev_id = all_docs[2 * rows - 1]
    dq, dk, dk_all = doc_ids[:, None], doc_ids[None, :], all_docs[None, :]

    log_decay = -(step * half(decay_rate, parity, 0)[None, :])
    total_decay = jnp.cumsum(log_decay, axis=0)
    final_sum = total_decay[-1]
    tail = jnp.exp(final_sum[None] - total_decay) * step
    tail = tail * (doc_ids == doc_ids[-1]).astype(F32)[:, None]
    entry = jnp.exp(total_decay) * (doc_ids == prev_id).astype(F32)[:, None]
    transmit = jnp.exp(final_sum) * (doc_ids[-1] == prev_id).astype(F32)

    def grouped(array):
        return jnp.transpose(array.reshape(rows, groups, group_heads), (1, 0, 2))

    def grouped_rows(array):
        return array.T.reshape(groups, group_heads, rows)

    width = x.shape[1] // groups
    state = b.shape[1] // groups
    col = pl.BlockSpec((rows, width), lambda g: (0, g))
    proj = pl.BlockSpec((rows, state), lambda g: (0, g))
    head_cols = pl.BlockSpec((1, rows, group_heads), lambda g: (g, 0, 0))
    head_rows = pl.BlockSpec((1, group_heads, rows), lambda g: (g, 0, 0))
    state_spec = pl.BlockSpec((state, width), lambda g: (0, g))
    row_spec = pl.BlockSpec((1, width), lambda g: (0, g))
    dq_spec = pl.BlockSpec((rows, 1), lambda g: (0, 0))
    dk_spec = pl.BlockSpec((1, rows), lambda g: (0, 0))

    states = []
    tail_g = grouped(tail)
    for g in range(groups):
        states.append(
            pl.pallas_call(
                state_kernel,
                grid=(1,),
                in_specs=[
                    pl.BlockSpec((rows, width), lambda _, g=g: (0, g)),
                    pl.BlockSpec((rows, state), lambda _, g=g: (0, g)),
                    pl.BlockSpec((1, rows, group_heads), lambda _, g=g: (g, 0, 0)),
                ],
                out_specs=pl.BlockSpec((state, width), lambda _: (0, 0)),
                out_shape=jax.ShapeDtypeStruct((state, width), BF16),
                scratch_shapes=[pltpu.VMEM((rows, width), BF16)],
                cost_estimate=pl.CostEstimate(
                    flops=2 * rows * state * width,
                    bytes_accessed=2 * (2 * rows * width),
                    transcendentals=0,
                ),
            )(x, b, tail_g)
        )
    far_kv = skipped(kv)
    near_kv = crossed(kv, far_kv)
    row = transmit[None, :]
    near_t = lax.ppermute(row, "ctx", [(j, j + 2) for j in range(n - 2)])
    far_states = [skipped(s) for s in states]
    near_states = [crossed(s, f) for s, f in zip(states, far_states)]

    total_l = grouped(total_decay)
    intra = pl.pallas_call(
        intra_kernel,
        grid=(groups,),
        in_specs=[col, proj, proj, head_cols, head_rows, head_rows, dq_spec, dk_spec],
        out_specs=col,
        out_shape=jax.ShapeDtypeStruct((rows, groups * width), F32),
        cost_estimate=pl.CostEstimate(
            flops=2 * rows * rows * groups * width * 2,
            bytes_accessed=8 * rows * groups * width,
            transcendentals=rows * rows * heads,
        ),
    )(x, b, c, total_l, grouped_rows(total_decay), grouped_rows(step), dq, dk)

    kv_heads = kv_width // ATT_DIM
    q_width = q.shape[1] // kv_heads

    def key_spec(k):
        return pl.BlockSpec((rows, ATT_DIM), lambda h: (0, h + k))

    attended = pl.pallas_call(
        attention_kernel,
        grid=(kv_heads,),
        in_specs=[pl.BlockSpec((rows, q_width), lambda h: (0, h))]
        + [key_spec(0), key_spec(kv_heads)] * 3
        + [dq_spec, pl.BlockSpec((1, 3 * rows), lambda h: (0, 0))],
        out_specs=pl.BlockSpec((rows, q_width), lambda h: (0, h)),
        out_shape=jax.ShapeDtypeStruct(q.shape, BF16),
        cost_estimate=pl.CostEstimate(
            flops=4 * rows * 3 * rows * q.shape[1],
            bytes_accessed=4 * rows * q.shape[1],
            transcendentals=rows * 3 * rows * q.shape[1] // ATT_DIM,
        ),
    )(q, far_kv, far_kv, near_kv, near_kv, kv, kv, dq, dk_all)

    head_size = width // group_heads
    wide_t = jnp.repeat(near_t, head_size, axis=1)
    weight = half(norm_weight, parity, 0)[None, :]
    entry_g = grouped(entry)
    tp_size = lax.axis_size("tp")
    part = rows // 4
    rank = parity * tp_size + tp_index

    def exchanged(block):
        pieces = block.reshape(4, part, block.shape[1])
        got = [(rank, lax.dynamic_index_in_dim(pieces, rank, 0, keepdims=False))]
        for flip_ctx, flip_tp in ((0, 1), (1, 1), (1, 0)):
            peer = (parity ^ flip_ctx) * tp_size + (tp_index ^ flip_tp)
            piece = lax.dynamic_index_in_dim(pieces, peer, 0, keepdims=False)
            route = [
                (i * tp_size + j, (i ^ flip_ctx) * tp_size + (j ^ flip_tp))
                for i in range(n)
                for j in range(tp_size)
            ]
            got.append((peer, lax.ppermute(piece, ("ctx", "tp"), route)))
        return got

    def placed(blocks):
        out = jnp.zeros((part, 4 * len(blocks) * blocks[0][0][1].shape[1]), BF16)
        for k, got in enumerate(blocks):
            for peer, piece in got:
                size = piece.shape[1]
                slot = (peer % tp_size) * 2 + peer // tp_size
                out = lax.dynamic_update_slice(out, piece, (0, (slot * len(blocks) + k) * size))
        return out

    attended_blocks = [exchanged(attended)]
    mixed_blocks = []
    for g in range(groups):
        at_g = lambda _, g=g: (0, g)
        mixed_g = pl.pallas_call(
            finish_kernel,
            grid=(1,),
            in_specs=[
                pl.BlockSpec((rows, width), at_g),
                pl.BlockSpec((rows, state), at_g),
                pl.BlockSpec((state, width), lambda _: (0, 0)),
                pl.BlockSpec((state, width), lambda _: (0, 0)),
                pl.BlockSpec((1, width), at_g),
                pl.BlockSpec((1, rows, group_heads), lambda _, g=g: (g, 0, 0)),
                pl.BlockSpec((rows, width), at_g),
                pl.BlockSpec((1, width), at_g),
            ],
            out_specs=pl.BlockSpec((rows, width), lambda _: (0, 0)),
            out_shape=jax.ShapeDtypeStruct((rows, width), BF16),
            scratch_shapes=[pltpu.VMEM((rows, width), F32)],
            cost_estimate=pl.CostEstimate(
                flops=2 * rows * state * width,
                bytes_accessed=12 * rows * width,
                transcendentals=rows * width,
            ),
        )(intra, c, near_states[g], far_states[g], wide_t, entry_g, gate, weight)
        mixed_blocks.append(exchanged(mixed_g))
    return (placed(mixed_blocks), placed(attended_blocks))


def solution(mesh):
    tp = mesh.shape["tp"]
    paired = tp == 2 and mesh.shape["ctx"] % 4 == 0 and GROUPS // tp % 2 == 0
    return jax.shard_map(
        local_pair if paired else local_any,
        mesh=mesh,
        in_specs=(
            P(),
            P("ctx", "tp"),
            P("ctx", "tp"),
            P("ctx", "tp"),
            P("ctx", "tp"),
            P("ctx", "tp"),
            P("tp"),
            P("tp"),
            P("ctx", "tp"),
            P("ctx", "tp"),
            P("ctx", "tp"),
        ),
        out_specs=(P(("ctx", "tp"), None), P(("ctx", "tp"), None)),
        check_vma=False,
    )
```

```python
import functools

import jax
import jax.numpy as jnp
from jax import lax
from jax.experimental import pallas as pl
from jax.experimental.pallas import tpu as pltpu
from jax.sharding import PartitionSpec as P

HEADS = 128
GROUPS = 8
ATT_DIM = 128
DOC_DEVS = 4


NEG_LARGE = -1e30


def for_sending(x):
    return jax.tree.map(lambda a: a.astype(jnp.bfloat16) if a.dtype == jnp.float32 else a, x)


def passed_along(block, axis, distance):
    devices = range(lax.axis_size(axis))
    route = [(i - distance, i) for i in devices if i - distance in devices]
    return lax.ppermute(block, axis, route)


def doc_starts(doc_lengths):
    return jnp.cumsum(doc_lengths) - doc_lengths


def doc_index(positions, starts):
    return jnp.sum((starts[None, :] <= positions[:, None]).astype(jnp.int32), axis=1) - 1


def block_terms(ssm_x, ssm_b, ssm_c, step_size, decay_rate, doc_ids, prev_id, group_heads):
    tok_rows = ssm_x.shape[0]
    head_count = step_size.shape[1]
    group_count = head_count // group_heads
    head_size = ssm_x.shape[1] // head_count
    state_size = ssm_b.shape[1] // group_count
    inputs = ssm_x.reshape(tok_rows, group_count, group_heads, head_size)
    in_proj = ssm_b.reshape(tok_rows, group_count, state_size)
    out_proj = ssm_c.reshape(tok_rows, group_count, state_size)
    log_decay = -(step_size * decay_rate[None, :])
    cumulative = jnp.cumsum(log_decay, axis=0)
    same_doc = doc_ids[:, None] == doc_ids[None, :]
    causal = jnp.arange(tok_rows)[:, None] >= jnp.arange(tok_rows)[None, :]
    allowed = (same_doc & causal)[None]
    spread = cumulative.T[:, :, None] - cumulative.T[:, None, :]
    weights = (
        jnp.where(allowed, jnp.exp(jnp.where(allowed, spread, 0.0)), 0.0) * step_size.T[:, None, :]
    )
    intersection = jnp.einsum("tgn,sgn->gts", out_proj, in_proj, preferred_element_type=jnp.float32)
    mixing = (
        weights.reshape(group_count, group_heads, tok_rows, tok_rows) * intersection[:, None]
    ).astype(jnp.bfloat16)
    y_intra = jnp.einsum("ghts,sghp->tghp", mixing, inputs, preferred_element_type=jnp.float32)
    final_sum = cumulative[-1]
    tail = (
        jnp.exp(final_sum[None, :] - cumulative)
        * step_size
        * (doc_ids == doc_ids[-1]).astype(jnp.float32)[:, None]
    )
    scaled = (
        inputs.astype(jnp.float32) * tail.reshape(tok_rows, group_count, group_heads)[..., None]
    ).astype(jnp.bfloat16)
    state_local = jnp.einsum("sghp,sgn->ghpn", scaled, in_proj, preferred_element_type=jnp.float32)
    entry = jnp.exp(cumulative) * (doc_ids == prev_id).astype(jnp.float32)[:, None]
    transmit = jnp.exp(final_sum) * (doc_ids[-1] == prev_id).astype(jnp.float32)
    return (y_intra, state_local, entry, transmit.reshape(group_count, group_heads))


def finish_rows(y_intra, entry, carried, ssm_c, ssm_gate, norm_weight):
    tok_rows, group_count, group_heads, head_size = y_intra.shape
    out_proj = ssm_c.reshape(tok_rows, group_count, -1).astype(jnp.float32)
    incoming = jnp.einsum("tgn,ghpn->tghp", out_proj, carried, precision=lax.Precision.HIGHEST)
    mixer_out = y_intra + incoming * entry.reshape(tok_rows, group_count, group_heads)[..., None]
    gate_vals = ssm_gate.reshape(tok_rows, group_count, group_heads, head_size).astype(jnp.float32)
    gated = (mixer_out * jax.nn.silu(gate_vals)).reshape(
        tok_rows, group_count, group_heads * head_size
    )
    factor = lax.rsqrt(jnp.mean(gated * gated, axis=2, keepdims=True) + 1e-05)
    return ((gated * factor).reshape(tok_rows, -1) * norm_weight[None, :]).astype(jnp.bfloat16)


def chain_states(earlier, later):
    return (earlier[0] * later[0], later[0][:, :, None, None] * earlier[1] + later[1])


def attention_update(
    carry, query_rows, key_block, value_block, key_pos, query_pos, query_doc, starts
):
    running_max, running_sum, running_acc = carry
    block_rows = key_block.shape[0]
    kv_local = key_block.shape[1] // ATT_DIM
    key_heads = key_block.reshape(block_rows, kv_local, ATT_DIM)
    value_heads = value_block.reshape(block_rows, kv_local, ATT_DIM)
    key_doc = doc_index(key_pos, starts)
    allowed = (query_doc[:, None] == key_doc[None, :]) & (key_pos[None, :] <= query_pos[:, None])
    scores = jnp.einsum(
        "tngd,knd->ngtk", query_rows, key_heads, preferred_element_type=jnp.float32
    ) * ATT_DIM ** (-0.5)
    scores = jnp.where(allowed[None, None], scores, -jnp.inf)
    new_max = jnp.maximum(running_max, jnp.max(scores, axis=3))
    probs = jnp.exp(scores - new_max[..., None])
    factor = jnp.exp(running_max - new_max)
    new_sum = running_sum * factor + jnp.sum(probs, axis=3)
    weighted = jnp.einsum(
        "ngtk,knd->ngtd",
        probs.astype(jnp.bfloat16),
        value_heads,
        preferred_element_type=jnp.float32,
    )
    return (new_max, new_sum, running_acc * factor[..., None] + weighted)


def local_any(
    doc_lengths,
    ssm_x,
    ssm_gate,
    ssm_b,
    ssm_c,
    step_size,
    decay_rate,
    norm_weight,
    queries,
    keys,
    values,
):
    tok_rows = ssm_x.shape[0]
    ctx_index = lax.axis_index("ctx")
    begin = ctx_index * tok_rows
    positions = begin + jnp.arange(tok_rows, dtype=jnp.int32)
    starts = doc_starts(doc_lengths)
    doc_ids = doc_index(positions, starts)
    prev_id = doc_index(jnp.reshape(begin - 1, (1,)), starts)[0]
    group_heads = HEADS // GROUPS
    y_intra, state_local, entry, transmit = block_terms(
        ssm_x, ssm_b, ssm_c, step_size, decay_rate, doc_ids, prev_id, group_heads
    )
    merged = (transmit, state_local)
    for level_bit in range(DOC_DEVS.bit_length() - 1):
        earlier = passed_along(
            (for_sending(merged[0]), for_sending(merged[1])), "ctx", 1 << level_bit
        )
        merged = chain_states(earlier, merged)
    carried = passed_along(merged[1], "ctx", 1)
    mixed_rows = finish_rows(y_intra, entry, carried, ssm_c, ssm_gate, norm_weight)
    kv_local = keys.shape[1] // ATT_DIM
    q_groups = queries.shape[1] // (kv_local * ATT_DIM)
    query_rows = queries.reshape(tok_rows, kv_local, q_groups, ATT_DIM)
    floor_start = jnp.max(jnp.where(starts <= begin, starts, 0))
    query_last = begin + tok_rows - 1
    carry_shape = (kv_local, q_groups, tok_rows)
    initial = (
        jnp.full(carry_shape, NEG_LARGE, jnp.float32),
        jnp.zeros(carry_shape, jnp.float32),
        jnp.zeros(carry_shape + (ATT_DIM,), jnp.float32),
    )

    def visit(carry, key_block, value_block, key_begin):
        block_rows = key_block.shape[0]
        needed = (key_begin <= query_last) & (key_begin + block_rows - 1 >= floor_start)

        def update(inner):
            key_pos = key_begin + jnp.arange(block_rows, dtype=jnp.int32)
            return attention_update(
                inner, query_rows, key_block, value_block, key_pos, positions, doc_ids, starts
            )

        def unchanged(inner):
            return inner

        return lax.cond(needed, update, unchanged, carry)

    totals = visit(initial, keys, values, begin)
    for hop_count in range(1, DOC_DEVS + 1):
        near_keys, near_values = passed_along((keys, values), "ctx", hop_count)
        totals = visit(totals, near_keys, near_values, begin - hop_count * tok_rows)
    final_out = totals[2] / totals[1][..., None]
    attended_rows = (
        jnp.transpose(final_out, (2, 0, 1, 3)).reshape(tok_rows, -1).astype(jnp.bfloat16)
    )
    mixed_local, attended_local = (
        lax.all_to_all(mixed_rows, "tp", split_axis=0, concat_axis=1, tiled=True),
        lax.all_to_all(attended_rows, "tp", split_axis=0, concat_axis=1, tiled=True),
    )
    return (mixed_local, attended_local)


LOG2E = 1.4426950408889634
F32 = jnp.float32
BF16 = jnp.bfloat16
MESH_ID = pl.DeviceIdType.MESH
COLS_LAST = (((1,), (1,)), ((), ()))
ROWS_FIRST = (((0,), (0,)), ((), ()))
PIECES = 2


def dot(a, b, dims=(((1,), (0,)), ((), ())), precision=None):
    return lax.dot_general(a, b, dims, precision=precision, preferred_element_type=F32)


def spread_heads(columns, head, head_size):
    lane = lax.broadcasted_iota(jnp.int32, (columns.shape[0], 128), 1)
    wide = jnp.broadcast_to(columns[:, head : head + 1], lane.shape)
    for k in range(1, 128 // head_size):
        wide = jnp.where(lane >= k * head_size, columns[:, head + k : head + k + 1], wide)
    return wide


def pair_kernel(
    n,
    lengths,
    x_in,
    gate_in,
    b_in,
    c_in,
    step_in,
    q_in,
    k_in,
    v_in,
    rate_ref,
    weight_ref,
    mixed_out,
    attended_out,
    x_s,
    gate_s,
    b_s,
    c_s,
    step_s,
    q_s,
    k_s,
    v_s,
    s_own,
    s_far,
    s_near,
    t_own,
    t_far,
    t_near,
    y_s,
    mixed_s,
    attended_s,
    bias_s,
    l_s,
    lt_s,
    dtt_s,
    tail_s,
    entry_s,
    send_sem,
    recv_sem,
    own_sem,
):
    index = lax.axis_index("ctx")
    tp = lax.axis_index("tp")
    parity, pair = lax.rem(index, 2), lax.div(index, 2)
    odd = lax.rem(pair, 2)
    base = index - parity
    other = 1 - parity
    tok = x_in.shape[0]
    rows = 2 * tok
    width = x_s.shape[1]
    group_heads = HEADS // GROUPS
    heads = step_in.shape[1] // 2
    groups = heads // group_heads
    group_width = width // groups
    state = b_s.shape[1] // groups
    head_size = width // heads
    kv_heads = k_s.shape[1] // ATT_DIM
    q_width = q_s.shape[1] // kv_heads
    piece = group_width // PIECES

    peers = [
        (base + other, tp),
        (index, 1 - tp),
        (base + other, 1 - tp),
        (index + 2 - 4 * odd, tp),
        (lax.rem(index + 4, n), tp),
        (lax.rem(index + n - 4, n), tp),
    ]
    ahead, behind = index + 4 < n, index >= 4
    barrier = pltpu.get_barrier_semaphore()
    for peer in peers:
        pl.semaphore_signal(barrier, inc=1, device_id=peer, device_id_type=MESH_ID)
    pl.semaphore_wait(barrier, len(peers))

    used = [0, 0]

    def slot():
        used[0] += 1
        return used[0] - 1

    def remote(src, dst, peer, k):
        return pltpu.make_async_remote_copy(
            src_ref=src,
            dst_ref=dst,
            send_sem=send_sem.at[k],
            recv_sem=recv_sem.at[k],
            device_id=peer,
            device_id_type=MESH_ID,
        )

    def kept(src, dst):
        used[1] += 1
        copy = pltpu.make_async_copy(src, dst, own_sem.at[used[1] - 1])
        copy.start()
        return copy

    mine = pl.ds(pl.multiple_of(parity * tok, tok), tok)
    sent = []

    def swap(src, dst, cols=None, skip=0):
        if cols is None:
            give, keep, place = src, src, dst.at[pl.ds(pl.multiple_of(parity * tok + skip, tok), tok)]
        else:
            begin, size, total = cols
            give = src.at[:, pl.ds(pl.multiple_of(other * total + begin, 128), size)]
            keep = src.at[:, pl.ds(pl.multiple_of(parity * total + begin, 128), size)]
            at = pl.ds(pl.multiple_of(parity * tok + skip, tok), tok)
            place = dst.at[at, begin : begin + size]
        copy = remote(give, place, peers[0], slot())
        copy.start()
        sent.append(copy)
        own = kept(keep, place)

        def ready():
            own.wait()
            copy.wait_recv()

        return ready

    kv_width = k_s.shape[1]
    ready_k = swap(k_in, k_s, (0, kv_width, kv_width), 2 * rows)
    ready_v = swap(v_in, v_s, (0, kv_width, kv_width), 2 * rows)
    ready_step = swap(step_in, step_s)
    ready_b = swap(b_in, b_s, (0, b_s.shape[1], b_s.shape[1]))
    ready_x = [swap(x_in, x_s, (g * group_width, group_width, width)) for g in range(groups)]
    ready_c = swap(c_in, c_s, (0, c_s.shape[1], c_s.shape[1]))
    ready_q = swap(q_in, q_s, (0, q_s.shape[1], q_s.shape[1]))
    ready_gate = swap(gate_in, gate_s, (0, width, width))

    first_pairs = pair < 2

    @pl.when(first_pairs)
    def _():
        k_s[:rows, :] = jnp.zeros((rows, kv_width), BF16)
        v_s[:rows, :] = jnp.zeros((rows, kv_width), BF16)
        s_far[...] = jnp.zeros_like(s_far)
        t_far[...] = jnp.zeros_like(t_far)

    def travel(own, far, near):
        far_slot, near_slot = slot(), slot()
        to_far = remote(own, far, (index + 4, tp), far_slot)
        direct = remote(own, near, peers[3], near_slot)
        relayed = remote(far, near, peers[3], near_slot)

        def start():
            @pl.when(ahead)
            def _():
                to_far.start()

            @pl.when(odd == 0)
            def _():
                direct.start()

        def relay():
            @pl.when(behind)
            def _():
                to_far.wait_recv()

            @pl.when(odd == 1)
            def _():
                relayed.start()

        def arrive():
            direct.wait_recv()

        def close():
            @pl.when(ahead)
            def _():
                to_far.wait_send()

            direct.wait_send()

        return start, relay, arrive, close

    own_rows = pl.ds(2 * rows, rows)
    k_trip = travel(k_s.at[own_rows], k_s.at[pl.ds(0, rows)], k_s.at[pl.ds(rows, rows)])
    v_trip = travel(v_s.at[own_rows], v_s.at[pl.ds(0, rows)], v_s.at[pl.ds(rows, rows)])
    t_trip = travel(t_own, t_far, t_near)
    trips = []
    for k in range(groups * PIECES):
        trips.append(travel(s_own.at[k], s_far.at[k], s_near.at[k]))

    ready_k()
    k_trip[0]()
    ready_v()
    v_trip[0]()

    begin = pair * rows
    row_at = begin - 2 * rows + lax.broadcasted_iota(jnp.int32, (1, 3 * rows), 1)
    col_at = begin + lax.broadcasted_iota(jnp.int32, (rows, 1), 0)
    row_doc = jnp.zeros_like(row_at) - 1
    col_doc = jnp.zeros_like(col_at) - 1
    begun, prev_id, last_id = jnp.int32(0), jnp.int32(-1), jnp.int32(-1)
    for j in range(lengths.shape[0]):
        row_doc += (row_at >= begun).astype(jnp.int32)
        col_doc += (col_at >= begun).astype(jnp.int32)
        prev_id += (begin - 1 >= begun).astype(jnp.int32)
        last_id += (begin + rows - 1 >= begun).astype(jnp.int32)
        begun = begun + lengths[j]
    bias_s[...] = jnp.where((row_doc == col_doc) & (row_at <= col_at), 0.0, NEG_LARGE)

    ready_step()
    low = parity == 0
    pad = jnp.zeros((rows, 128 - heads), F32)
    step = jnp.concatenate([jnp.where(low, step_s[:, :heads], step_s[:, heads:]), pad], axis=1)
    rate = jnp.where(low, rate_ref[:, :heads], rate_ref[:, heads:])
    rate = jnp.concatenate([rate, pad[:1]], axis=1)
    at = lax.broadcasted_iota(jnp.int32, (rows, rows), 0)
    to = lax.broadcasted_iota(jnp.int32, (rows, rows), 1)
    lower = (to <= at).astype(F32)
    total_decay = dot(lower, -(step * rate), precision=lax.Precision.HIGHEST)
    final_sum = total_decay[rows - 1 :, :]
    l_s[...] = total_decay
    lt_s[...] = total_decay.T
    dtt_s[...] = step.T
    tail_s[...] = jnp.where(col_doc == last_id, jnp.exp(final_sum - total_decay) * step, 0.0)
    entry_s[...] = jnp.where(col_doc == prev_id, jnp.exp(total_decay), 0.0)
    passing = (last_id == prev_id).astype(F32)
    t_own[...] = jnp.broadcast_to(jnp.exp(final_sum) * passing, t_own.shape)
    t_trip[0]()

    per = 128 // head_size
    ready_b()
    for g in range(groups):
        ready_x[g]()
        b_t = b_s[:, g * state : (g + 1) * state].T
        for p in range(PIECES):
            parts = []
            for tile in range(piece // 128):
                lead = g * group_width + p * piece + tile * 128
                wide = spread_heads(tail_s[...], lead // head_size, head_size)
                parts.append((x_s[:, lead : lead + 128].astype(F32) * wide).astype(BF16))
            s_own[g * PIECES + p] = dot(b_t, jnp.concatenate(parts, axis=1)).astype(BF16)
            trips[g * PIECES + p][0]()

    lane = lax.broadcasted_iota(jnp.int32, (rows, 128), 1)
    ready_c()
    for g in range(groups):
        proj = slice(g * state, (g + 1) * state)
        inter = dot(c_s[:, proj], b_s[:, proj], COLS_LAST)
        for tile in range(group_width // 128):
            lead = g * group_width + tile * 128
            for k in range(per):
                h = lead // head_size + k
                spread = l_s[:, h : h + 1] - lt_s[h : h + 1, :]
                w = jnp.exp(spread + bias_s[:, 2 * rows :]) * dtt_s[h : h + 1, :]
                part = dot((w * inter).astype(BF16), x_s[:, lead : lead + 128])
                whole = part if k == 0 else jnp.where(lane >= k * head_size, part, whole)
            y_s[:, lead : lead + 128] = whole
        if g == 0:
            k_trip[1]()
            v_trip[1]()

    part_rows = rows // 4
    leaving = []

    def exchange(src, out, g, size):
        home = pl.ds(pl.multiple_of((tp * 2 + parity) * groups * size + g * size, 128), size)
        cols = slice(g * size, (g + 1) * size)
        for peer, fc, ft in ((peers[1], 0, 1), (peers[2], 1, 1), (peers[0], 1, 0)):
            rank = (other if fc else parity) * 2 + (1 - tp if ft else tp)
            at_rows = pl.ds(pl.multiple_of(rank * part_rows, part_rows), part_rows)
            copy = remote(src.at[at_rows, cols], out.at[:, home], peer, slot())
            copy.start()
            leaving.append(copy)
        at_rows = pl.ds(pl.multiple_of((parity * 2 + tp) * part_rows, part_rows), part_rows)
        leaving.append(kept(src.at[at_rows, cols], out.at[:, home]))

    scale = LOG2E * ATT_DIM ** (-0.5)
    ready_q()
    k_trip[2]()
    v_trip[2]()
    for kv_head in range(kv_heads):
        kv_cols = slice(kv_head * ATT_DIM, (kv_head + 1) * ATT_DIM)

        def one_head(h, carry):
            cols = pl.ds(pl.multiple_of(kv_head * q_width + h * ATT_DIM, ATT_DIM), ATT_DIM)
            scores = dot(q_s[:, cols], k_s[:, kv_cols], COLS_LAST) + bias_s[...]
            top = jnp.max(scores, axis=1, keepdims=True)
            probs = jnp.exp2((scores - top) * scale)
            total = jnp.sum(probs, axis=1, keepdims=True)
            summed = dot(probs.astype(BF16), v_s[:, kv_cols])
            attended_s[:, cols] = (summed / total).astype(BF16)
            return carry

        lax.fori_loop(0, q_width // ATT_DIM, one_head, 0)
        exchange(attended_s, attended_out, kv_head, q_width)
        if kv_head == 0:
            t_trip[1]()
            trips[0][1]()
        else:
            trips[1][1]()

    ready_gate()
    t_trip[2]()
    for g in range(groups):
        proj = slice(g * state, (g + 1) * state)
        square = jnp.zeros((rows, 128), F32)
        for p in range(PIECES):
            k = g * PIECES + p
            if k >= 2:
                trips[k][1]()
            trips[k][2]()
            lead = g * group_width + p * piece
            decay = jnp.concatenate(
                [
                    spread_heads(t_near[...], (lead + tile * 128) // head_size, head_size)[:1]
                    for tile in range(piece // 128)
                ],
                axis=1,
            )
            carried = (s_near[k].astype(F32) + decay * s_far[k].astype(F32)).astype(BF16)
            incoming = dot(c_s[:, proj], carried)
            for tile in range(piece // 128):
                cols = slice(lead + tile * 128, lead + tile * 128 + 128)
                wide = spread_heads(entry_s[...], (lead + tile * 128) // head_size, head_size)
                z = gate_s[:, cols].astype(F32)
                total = y_s[:, cols] + incoming[:, tile * 128 : tile * 128 + 128] * wide
                total = total * (z / (1.0 + jnp.exp(-z)))
                y_s[:, cols] = total
                square += total * total
        mean = jnp.sum(square, axis=1, keepdims=True) * (1.0 / group_width)
        factor = lax.rsqrt(mean + 1e-05)
        for tile in range(group_width // 128):
            lead = g * group_width + tile * 128
            cols = slice(lead, lead + 128)
            gain = jnp.where(low, weight_ref[:, cols], weight_ref[:, lead + width : lead + width + 128])
            mixed_s[:, cols] = (y_s[:, cols] * factor * gain).astype(BF16)
        exchange(mixed_s, mixed_out, g, group_width)

    for copy in sent:
        copy.wait_send()
    for trip in [k_trip, v_trip, t_trip] + trips:
        trip[3]()
    for copy in leaving:
        copy.wait()


def local_pair(
    doc_lengths,
    ssm_x,
    ssm_gate,
    ssm_b,
    ssm_c,
    step_size,
    decay_rate,
    norm_weight,
    queries,
    keys,
    values,
):
    tok, width = ssm_x.shape
    rows, half = 2 * tok, width // 2
    groups = step_size.shape[1] * GROUPS // HEADS // 2
    state = ssm_b.shape[1] // (2 * groups)
    piece = half // groups // PIECES
    kv_half = keys.shape[1] // 2
    q_half = queries.shape[1] // 2
    pieces = groups * PIECES
    copies = 9 + groups - 1 + 6 + 2 * pieces + 12
    any_spec = pl.BlockSpec(memory_space=pl.ANY)
    vmem_spec = pl.BlockSpec(memory_space=pltpu.VMEM)
    part = rows // 4
    scratch = [
        pltpu.VMEM((rows, half), BF16),
        pltpu.VMEM((rows, half), BF16),
        pltpu.VMEM((rows, groups * state), BF16),
        pltpu.VMEM((rows, groups * state), BF16),
        pltpu.VMEM((rows, step_size.shape[1]), F32),
        pltpu.VMEM((rows, q_half), BF16),
        pltpu.VMEM((3 * rows, kv_half), BF16),
        pltpu.VMEM((3 * rows, kv_half), BF16),
        pltpu.VMEM((pieces, state, piece), BF16),
        pltpu.VMEM((pieces, state, piece), BF16),
        pltpu.VMEM((pieces, state, piece), BF16),
        pltpu.VMEM((8, 128), F32),
        pltpu.VMEM((8, 128), F32),
        pltpu.VMEM((8, 128), F32),
        pltpu.VMEM((rows, half), F32),
        pltpu.VMEM((rows, half), BF16),
        pltpu.VMEM((rows, q_half), BF16),
        pltpu.VMEM((rows, 3 * rows), F32),
        pltpu.VMEM((rows, 128), F32),
        pltpu.VMEM((128, rows), F32),
        pltpu.VMEM((128, rows), F32),
        pltpu.VMEM((rows, 128), F32),
        pltpu.VMEM((rows, 128), F32),
        pltpu.SemaphoreType.DMA((copies,)),
        pltpu.SemaphoreType.DMA((copies,)),
        pltpu.SemaphoreType.DMA((copies,)),
    ]
    mixed, attended = pl.pallas_call(
        functools.partial(pair_kernel, lax.axis_size("ctx")),
        out_shape=(
            jax.ShapeDtypeStruct((part, 4 * half), BF16),
            jax.ShapeDtypeStruct((part, 4 * q_half), BF16),
        ),
        in_specs=[pl.BlockSpec(memory_space=pltpu.SMEM)] + [any_spec] * 8 + [vmem_spec] * 2,
        out_specs=(any_spec, any_spec),
        scratch_shapes=scratch,
        compiler_params=pltpu.CompilerParams(collective_id=0, has_side_effects=True),
    )(
        doc_lengths,
        ssm_x,
        ssm_gate,
        ssm_b,
        ssm_c,
        step_size,
        queries,
        keys,
        values,
        decay_rate[None, :],
        norm_weight[None, :],
    )
    return (mixed, attended)


def solution(mesh):
    tp = mesh.shape["tp"]
    paired = tp == 2 and mesh.shape["ctx"] % 4 == 0 and mesh.shape["ctx"] > 4 and GROUPS // tp % 2 == 0
    return jax.shard_map(
        local_pair if paired else local_any,
        mesh=mesh,
        in_specs=(
            P(),
            P("ctx", "tp"),
            P("ctx", "tp"),
            P("ctx", "tp"),
            P("ctx", "tp"),
            P("ctx", "tp"),
            P("tp"),
            P("tp"),
            P("ctx", "tp"),
            P("ctx", "tp"),
            P("ctx", "tp"),
        ),
        out_specs=(P(("ctx", "tp"), None), P(("ctx", "tp"), None)),
        check_vma=False,
    )
```

```python
import functools

import jax
import jax.numpy as jnp
from jax import lax
from jax.experimental import pallas as pl
from jax.experimental.pallas import tpu as pltpu
from jax.sharding import PartitionSpec as P

HEADS = 128
GROUPS = 8
ATT_DIM = 128
DOC_DEVS = 4


NEG_LARGE = -1e30


def for_sending(x):
    return jax.tree.map(lambda a: a.astype(jnp.bfloat16) if a.dtype == jnp.float32 else a, x)


def passed_along(block, axis, distance):
    devices = range(lax.axis_size(axis))
    route = [(i - distance, i) for i in devices if i - distance in devices]
    return lax.ppermute(block, axis, route)


def doc_starts(doc_lengths):
    return jnp.cumsum(doc_lengths) - doc_lengths


def doc_index(positions, starts):
    return jnp.sum((starts[None, :] <= positions[:, None]).astype(jnp.int32), axis=1) - 1


def block_terms(ssm_x, ssm_b, ssm_c, step_size, decay_rate, doc_ids, prev_id, group_heads):
    tok_rows = ssm_x.shape[0]
    head_count = step_size.shape[1]
    group_count = head_count // group_heads
    head_size = ssm_x.shape[1] // head_count
    state_size = ssm_b.shape[1] // group_count
    inputs = ssm_x.reshape(tok_rows, group_count, group_heads, head_size)
    in_proj = ssm_b.reshape(tok_rows, group_count, state_size)
    out_proj = ssm_c.reshape(tok_rows, group_count, state_size)
    log_decay = -(step_size * decay_rate[None, :])
    cumulative = jnp.cumsum(log_decay, axis=0)
    same_doc = doc_ids[:, None] == doc_ids[None, :]
    causal = jnp.arange(tok_rows)[:, None] >= jnp.arange(tok_rows)[None, :]
    allowed = (same_doc & causal)[None]
    spread = cumulative.T[:, :, None] - cumulative.T[:, None, :]
    weights = (
        jnp.where(allowed, jnp.exp(jnp.where(allowed, spread, 0.0)), 0.0) * step_size.T[:, None, :]
    )
    intersection = jnp.einsum("tgn,sgn->gts", out_proj, in_proj, preferred_element_type=jnp.float32)
    mixing = (
        weights.reshape(group_count, group_heads, tok_rows, tok_rows) * intersection[:, None]
    ).astype(jnp.bfloat16)
    y_intra = jnp.einsum("ghts,sghp->tghp", mixing, inputs, preferred_element_type=jnp.float32)
    final_sum = cumulative[-1]
    tail = (
        jnp.exp(final_sum[None, :] - cumulative)
        * step_size
        * (doc_ids == doc_ids[-1]).astype(jnp.float32)[:, None]
    )
    scaled = (
        inputs.astype(jnp.float32) * tail.reshape(tok_rows, group_count, group_heads)[..., None]
    ).astype(jnp.bfloat16)
    state_local = jnp.einsum("sghp,sgn->ghpn", scaled, in_proj, preferred_element_type=jnp.float32)
    entry = jnp.exp(cumulative) * (doc_ids == prev_id).astype(jnp.float32)[:, None]
    transmit = jnp.exp(final_sum) * (doc_ids[-1] == prev_id).astype(jnp.float32)
    return (y_intra, state_local, entry, transmit.reshape(group_count, group_heads))


def finish_rows(y_intra, entry, carried, ssm_c, ssm_gate, norm_weight):
    tok_rows, group_count, group_heads, head_size = y_intra.shape
    out_proj = ssm_c.reshape(tok_rows, group_count, -1).astype(jnp.float32)
    incoming = jnp.einsum("tgn,ghpn->tghp", out_proj, carried, precision=lax.Precision.HIGHEST)
    mixer_out = y_intra + incoming * entry.reshape(tok_rows, group_count, group_heads)[..., None]
    gate_vals = ssm_gate.reshape(tok_rows, group_count, group_heads, head_size).astype(jnp.float32)
    gated = (mixer_out * jax.nn.silu(gate_vals)).reshape(
        tok_rows, group_count, group_heads * head_size
    )
    factor = lax.rsqrt(jnp.mean(gated * gated, axis=2, keepdims=True) + 1e-05)
    return ((gated * factor).reshape(tok_rows, -1) * norm_weight[None, :]).astype(jnp.bfloat16)


def chain_states(earlier, later):
    return (earlier[0] * later[0], later[0][:, :, None, None] * earlier[1] + later[1])


def attention_update(
    carry, query_rows, key_block, value_block, key_pos, query_pos, query_doc, starts
):
    running_max, running_sum, running_acc = carry
    block_rows = key_block.shape[0]
    kv_local = key_block.shape[1] // ATT_DIM
    key_heads = key_block.reshape(block_rows, kv_local, ATT_DIM)
    value_heads = value_block.reshape(block_rows, kv_local, ATT_DIM)
    key_doc = doc_index(key_pos, starts)
    allowed = (query_doc[:, None] == key_doc[None, :]) & (key_pos[None, :] <= query_pos[:, None])
    scores = jnp.einsum(
        "tngd,knd->ngtk", query_rows, key_heads, preferred_element_type=jnp.float32
    ) * ATT_DIM ** (-0.5)
    scores = jnp.where(allowed[None, None], scores, -jnp.inf)
    new_max = jnp.maximum(running_max, jnp.max(scores, axis=3))
    probs = jnp.exp(scores - new_max[..., None])
    factor = jnp.exp(running_max - new_max)
    new_sum = running_sum * factor + jnp.sum(probs, axis=3)
    weighted = jnp.einsum(
        "ngtk,knd->ngtd",
        probs.astype(jnp.bfloat16),
        value_heads,
        preferred_element_type=jnp.float32,
    )
    return (new_max, new_sum, running_acc * factor[..., None] + weighted)


def local_any(
    doc_lengths,
    ssm_x,
    ssm_gate,
    ssm_b,
    ssm_c,
    step_size,
    decay_rate,
    norm_weight,
    queries,
    keys,
    values,
):
    tok_rows = ssm_x.shape[0]
    ctx_index = lax.axis_index("ctx")
    begin = ctx_index * tok_rows
    positions = begin + jnp.arange(tok_rows, dtype=jnp.int32)
    starts = doc_starts(doc_lengths)
    doc_ids = doc_index(positions, starts)
    prev_id = doc_index(jnp.reshape(begin - 1, (1,)), starts)[0]
    group_heads = HEADS // GROUPS
    y_intra, state_local, entry, transmit = block_terms(
        ssm_x, ssm_b, ssm_c, step_size, decay_rate, doc_ids, prev_id, group_heads
    )
    merged = (transmit, state_local)
    for level_bit in range(DOC_DEVS.bit_length() - 1):
        earlier = passed_along(
            (for_sending(merged[0]), for_sending(merged[1])), "ctx", 1 << level_bit
        )
        merged = chain_states(earlier, merged)
    carried = passed_along(merged[1], "ctx", 1)
    mixed_rows = finish_rows(y_intra, entry, carried, ssm_c, ssm_gate, norm_weight)
    kv_local = keys.shape[1] // ATT_DIM
    q_groups = queries.shape[1] // (kv_local * ATT_DIM)
    query_rows = queries.reshape(tok_rows, kv_local, q_groups, ATT_DIM)
    floor_start = jnp.max(jnp.where(starts <= begin, starts, 0))
    query_last = begin + tok_rows - 1
    carry_shape = (kv_local, q_groups, tok_rows)
    initial = (
        jnp.full(carry_shape, NEG_LARGE, jnp.float32),
        jnp.zeros(carry_shape, jnp.float32),
        jnp.zeros(carry_shape + (ATT_DIM,), jnp.float32),
    )

    def visit(carry, key_block, value_block, key_begin):
        block_rows = key_block.shape[0]
        needed = (key_begin <= query_last) & (key_begin + block_rows - 1 >= floor_start)

        def update(inner):
            key_pos = key_begin + jnp.arange(block_rows, dtype=jnp.int32)
            return attention_update(
                inner, query_rows, key_block, value_block, key_pos, positions, doc_ids, starts
            )

        def unchanged(inner):
            return inner

        return lax.cond(needed, update, unchanged, carry)

    totals = visit(initial, keys, values, begin)
    for hop_count in range(1, DOC_DEVS + 1):
        near_keys, near_values = passed_along((keys, values), "ctx", hop_count)
        totals = visit(totals, near_keys, near_values, begin - hop_count * tok_rows)
    final_out = totals[2] / totals[1][..., None]
    attended_rows = (
        jnp.transpose(final_out, (2, 0, 1, 3)).reshape(tok_rows, -1).astype(jnp.bfloat16)
    )
    mixed_local, attended_local = (
        lax.all_to_all(mixed_rows, "tp", split_axis=0, concat_axis=1, tiled=True),
        lax.all_to_all(attended_rows, "tp", split_axis=0, concat_axis=1, tiled=True),
    )
    return (mixed_local, attended_local)


LOG2E = 1.4426950408889634
F32 = jnp.float32
BF16 = jnp.bfloat16
MESH_ID = pl.DeviceIdType.MESH
COLS_LAST = (((1,), (1,)), ((), ()))
ROWS_FIRST = (((0,), (0,)), ((), ()))
PIECES = 4
SHARES = 2
RELAY_AFTER = (0, 2, 3, None)


def dot(a, b, dims=(((1,), (0,)), ((), ())), precision=None):
    return lax.dot_general(a, b, dims, precision=precision, preferred_element_type=F32)


def spread_heads(columns, head, head_size):
    lane = lax.broadcasted_iota(jnp.int32, (columns.shape[0], 128), 1)
    wide = jnp.broadcast_to(columns[:, head : head + 1], lane.shape)
    for k in range(1, 128 // head_size):
        wide = jnp.where(lane >= k * head_size, columns[:, head + k : head + k + 1], wide)
    return wide


def pair_kernel(
    n,
    lengths,
    x_in,
    gate_in,
    b_in,
    c_in,
    step_in,
    q_in,
    k_in,
    v_in,
    rate_ref,
    weight_ref,
    mixed_out,
    attended_out,
    x_s,
    gate_s,
    b_s,
    c_s,
    step_s,
    q_s,
    k_s,
    v_s,
    s_own,
    s_far,
    s_near,
    t_own,
    t_far,
    t_near,
    y_s,
    mixed_s,
    attended_s,
    bias_s,
    l_s,
    lt_s,
    dtt_s,
    tail_s,
    entry_s,
    send_sem,
    recv_sem,
    own_sem,
):
    index = lax.axis_index("ctx")
    tp = lax.axis_index("tp")
    parity, pair = lax.rem(index, 2), lax.div(index, 2)
    odd = lax.rem(pair, 2)
    base = index - parity
    other = 1 - parity
    tok = x_in.shape[0]
    rows = 2 * tok
    width = x_s.shape[1]
    group_heads = HEADS // GROUPS
    heads = step_in.shape[0] // 2
    groups = heads // group_heads
    group_width = width // groups
    state = b_s.shape[1] // groups
    head_size = width // heads
    kv_heads = k_s.shape[1] // ATT_DIM
    q_width = q_s.shape[1] // kv_heads
    piece = group_width // PIECES

    peers = [
        (base + other, tp),
        (index, 1 - tp),
        (base + other, 1 - tp),
        (index + 2 - 4 * odd, tp),
        (lax.rem(index + 4, n), tp),
        (lax.rem(index + n - 4, n), tp),
    ]
    ahead, behind = index + 4 < n, index >= 4
    barrier = pltpu.get_barrier_semaphore()
    for peer in peers:
        pl.semaphore_signal(barrier, inc=1, device_id=peer, device_id_type=MESH_ID)
    pl.semaphore_wait(barrier, len(peers))

    used = [0, 0]

    def slot():
        used[0] += 1
        return used[0] - 1

    def remote(src, dst, peer, k):
        return pltpu.make_async_remote_copy(
            src_ref=src,
            dst_ref=dst,
            send_sem=send_sem.at[k],
            recv_sem=recv_sem.at[k],
            device_id=peer,
            device_id_type=MESH_ID,
        )

    def kept(src, dst):
        used[1] += 1
        copy = pltpu.make_async_copy(src, dst, own_sem.at[used[1] - 1])
        copy.start()
        return copy

    mine = pl.ds(pl.multiple_of(parity * tok, tok), tok)
    sent = []

    def swap(src, dst, cols, skip=0):
        begin, size, total = cols
        give = src.at[:, pl.ds(pl.multiple_of(other * total + begin, 128), size)]
        keep = src.at[:, pl.ds(pl.multiple_of(parity * total + begin, 128), size)]
        at = pl.ds(pl.multiple_of(parity * tok + skip, tok), tok)
        place = dst.at[at, begin : begin + size]
        copy = remote(give, place, peers[0], slot())
        copy.start()
        sent.append(copy)
        own = kept(keep, place)

        def ready():
            own.wait()
            copy.wait_recv()

        return ready

    kv_width = k_s.shape[1]
    ready_k = swap(k_in, k_s, (0, kv_width, kv_width), 2 * rows)
    ready_v = swap(v_in, v_s, (0, kv_width, kv_width), 2 * rows)
    give_rows = pl.ds(pl.multiple_of(other * heads, 8), heads)
    keep_rows = pl.ds(pl.multiple_of(parity * heads, 8), heads)
    copy_step = remote(step_in.at[give_rows], step_s.at[:, mine], peers[0], slot())
    copy_step.start()
    sent.append(copy_step)
    own_step = kept(step_in.at[keep_rows], step_s.at[:, mine])
    ready_b = swap(b_in, b_s, (0, b_s.shape[1], b_s.shape[1]))
    ready_x = [swap(x_in, x_s, (g * group_width, group_width, width)) for g in range(groups)]

    first_pairs = pair < 2

    @pl.when(first_pairs)
    def _():
        k_s[:rows, :] = jnp.zeros((rows, kv_width), BF16)
        v_s[:rows, :] = jnp.zeros((rows, kv_width), BF16)
        s_far[...] = jnp.zeros_like(s_far)
        t_far[...] = jnp.zeros_like(t_far)

    def travel(own, far, near):
        far_slot, near_slot = slot(), slot()
        to_far = remote(own, far, (index + 4, tp), far_slot)
        direct = remote(own, near, peers[3], near_slot)
        relayed = remote(far, near, peers[3], near_slot)

        def start():
            @pl.when(ahead)
            def _():
                to_far.start()

            @pl.when(odd == 0)
            def _():
                direct.start()

        def relay():
            @pl.when(behind & (odd == 1))
            def _():
                to_far.wait_recv()

            @pl.when(odd == 1)
            def _():
                relayed.start()

        def arrive():
            @pl.when(behind & (odd == 0))
            def _():
                to_far.wait_recv()

            direct.wait_recv()

        def close():
            @pl.when(ahead)
            def _():
                to_far.wait_send()

            direct.wait_send()

        return start, relay, arrive, close

    own_rows = pl.ds(2 * rows, rows)
    k_trip = travel(k_s.at[own_rows], k_s.at[pl.ds(0, rows)], k_s.at[pl.ds(rows, rows)])
    v_trip = travel(v_s.at[own_rows], v_s.at[pl.ds(0, rows)], v_s.at[pl.ds(rows, rows)])
    t_trip = travel(t_own, t_far, t_near)
    trips = []
    for k in range(groups * PIECES):
        trips.append(travel(s_own.at[k], s_far.at[k], s_near.at[k]))

    ready_k()
    k_trip[0]()
    ready_v()
    v_trip[0]()

    begin = pair * rows
    row_at = begin - 2 * rows + lax.broadcasted_iota(jnp.int32, (1, 3 * rows), 1)
    col_at = begin + lax.broadcasted_iota(jnp.int32, (rows, 1), 0)
    row_doc = jnp.zeros_like(row_at) - 1
    col_doc = jnp.zeros_like(col_at) - 1
    begun, prev_id, last_id = jnp.int32(0), jnp.int32(-1), jnp.int32(-1)
    for j in range(lengths.shape[0]):
        row_doc += (row_at >= begun).astype(jnp.int32)
        col_doc += (col_at >= begun).astype(jnp.int32)
        prev_id += (begin - 1 >= begun).astype(jnp.int32)
        last_id += (begin + rows - 1 >= begun).astype(jnp.int32)
        begun = begun + lengths[j]
    bias_s[...] = jnp.where((row_doc == col_doc) & (row_at <= col_at), 0.0, NEG_LARGE)

    own_step.wait()
    copy_step.wait_recv()
    low = parity == 0
    pad = jnp.zeros((1, 128 - heads), F32)
    step_t = jnp.concatenate([step_s[...], jnp.zeros((128 - heads, rows), F32)], axis=0)
    step = step_t.T
    rate = jnp.where(low, rate_ref[:, :heads], rate_ref[:, heads:])
    rate = jnp.concatenate([rate, pad], axis=1)
    at = lax.broadcasted_iota(jnp.int32, (rows, rows), 0)
    to = lax.broadcasted_iota(jnp.int32, (rows, rows), 1)
    lower = (to <= at).astype(F32)
    total_decay = dot(lower, -(step * rate), precision=lax.Precision.HIGHEST)
    final_sum = total_decay[rows - 1 :, :]
    l_s[...] = total_decay
    lt_s[...] = total_decay.T
    dtt_s[...] = step_t
    tail_s[...] = jnp.where(col_doc == last_id, jnp.exp(final_sum - total_decay) * step, 0.0)
    entry_s[...] = jnp.where(col_doc == prev_id, jnp.exp(total_decay), 0.0)
    passing = (last_id == prev_id).astype(F32)
    t_own[...] = jnp.broadcast_to(jnp.exp(final_sum) * passing, t_own.shape)
    t_trip[0]()

    per = 128 // head_size
    ready_b()
    for g in range(groups):
        ready_x[g]()
        if g == groups - 1:
            ready_c = swap(c_in, c_s, (0, c_s.shape[1], c_s.shape[1]))
            ready_q = swap(q_in, q_s, (0, q_s.shape[1], q_s.shape[1]))
            ready_gate = swap(gate_in, gate_s, (0, width, width))
        b_t = b_s[:, g * state : (g + 1) * state].T
        for p in range(PIECES):
            parts = []
            for tile in range(piece // 128):
                lead = g * group_width + p * piece + tile * 128
                wide = spread_heads(tail_s[...], lead // head_size, head_size)
                parts.append((x_s[:, lead : lead + 128].astype(F32) * wide).astype(BF16))
            s_own[g * PIECES + p] = dot(b_t, jnp.concatenate(parts, axis=1)).astype(BF16)
            trips[g * PIECES + p][0]()
        (k_trip, v_trip)[g][1]()

    lane = lax.broadcasted_iota(jnp.int32, (rows, 128), 1)
    ready_c()
    for g in range(groups):
        proj = slice(g * state, (g + 1) * state)
        inter = dot(c_s[:, proj], b_s[:, proj], COLS_LAST)
        for tile in range(group_width // 128):
            lead = g * group_width + tile * 128
            for k in range(per):
                h = lead // head_size + k
                spread = l_s[:, h : h + 1] - lt_s[h : h + 1, :]
                w = jnp.exp(spread + bias_s[:, 2 * rows :]) * dtt_s[h : h + 1, :]
                part = dot((w * inter).astype(BF16), x_s[:, lead : lead + 128])
                whole = part if k == 0 else jnp.where(lane >= k * head_size, part, whole)
            y_s[:, lead : lead + 128] = whole
    part_rows = rows // 4
    leaving = []

    def exchange(src, out, g, size, count):
        home = pl.ds(pl.multiple_of((tp * 2 + parity) * count * size + g * size, 128), size)
        cols = slice(g * size, (g + 1) * size)
        for peer, fc, ft in ((peers[1], 0, 1), (peers[2], 1, 1), (peers[0], 1, 0)):
            rank = (other if fc else parity) * 2 + (1 - tp if ft else tp)
            at_rows = pl.ds(pl.multiple_of(rank * part_rows, part_rows), part_rows)
            copy = remote(src.at[at_rows, cols], out.at[:, home], peer, slot())
            copy.start()
            leaving.append(copy)
        at_rows = pl.ds(pl.multiple_of((parity * 2 + tp) * part_rows, part_rows), part_rows)
        leaving.append(kept(src.at[at_rows, cols], out.at[:, home]))

    scale = LOG2E * ATT_DIM ** (-0.5)
    ready_q()
    k_trip[2]()
    v_trip[2]()
    for kv_head in range(kv_heads):
        kv_cols = slice(kv_head * ATT_DIM, (kv_head + 1) * ATT_DIM)

        def one_head(h, carry):
            cols = pl.ds(pl.multiple_of(kv_head * q_width + h * ATT_DIM, ATT_DIM), ATT_DIM)
            scores = dot(q_s[:, cols], k_s[:, kv_cols], COLS_LAST) + bias_s[...]
            top = jnp.max(scores, axis=1, keepdims=True)
            probs = jnp.exp2((scores - top) * scale)
            total = jnp.sum(probs, axis=1, keepdims=True)
            summed = dot(probs.astype(BF16), v_s[:, kv_cols])
            attended_s[:, cols] = (summed / total).astype(BF16)
            return carry

        span = q_width // ATT_DIM // SHARES
        for share in range(SHARES):
            lax.fori_loop(share * span, (share + 1) * span, one_head, 0, unroll=2)
            exchange(attended_s, attended_out, kv_head * SHARES + share, q_width // SHARES, kv_heads * SHARES)
            done = kv_head * SHARES + share
            if done == 0:
                t_trip[1]()
            for k in range(len(trips)):
                if RELAY_AFTER[k * 4 // len(trips)] == done:
                    trips[k][1]()

    ready_gate()
    t_trip[2]()
    for g in range(groups):
        proj = slice(g * state, (g + 1) * state)
        square = jnp.zeros((rows, 128), F32)
        for p in range(PIECES):
            k = g * PIECES + p
            if RELAY_AFTER[k * 4 // len(trips)] is None:
                trips[k][1]()
            trips[k][2]()
            lead = g * group_width + p * piece
            decay = jnp.concatenate(
                [
                    spread_heads(t_near[...], (lead + tile * 128) // head_size, head_size)[:1]
                    for tile in range(piece // 128)
                ],
                axis=1,
            )
            carried = (s_near[k].astype(F32) + decay * s_far[k].astype(F32)).astype(BF16)
            incoming = dot(c_s[:, proj], carried)
            for tile in range(piece // 128):
                cols = slice(lead + tile * 128, lead + tile * 128 + 128)
                wide = spread_heads(entry_s[...], (lead + tile * 128) // head_size, head_size)
                z = gate_s[:, cols].astype(F32)
                total = y_s[:, cols] + incoming[:, tile * 128 : tile * 128 + 128] * wide
                total = total * (z / (1.0 + jnp.exp(-z)))
                y_s[:, cols] = total
                square += total * total
        mean = jnp.sum(square, axis=1, keepdims=True) * (1.0 / group_width)
        factor = lax.rsqrt(mean + 1e-05)
        for tile in range(group_width // 128):
            lead = g * group_width + tile * 128
            cols = slice(lead, lead + 128)
            gain = jnp.where(low, weight_ref[:, cols], weight_ref[:, lead + width : lead + width + 128])
            mixed_s[:, cols] = (y_s[:, cols] * factor * gain).astype(BF16)
        exchange(mixed_s, mixed_out, g, group_width, groups)

    for copy in sent:
        copy.wait_send()
    for trip in [k_trip, v_trip, t_trip] + trips:
        trip[3]()
    for copy in leaving:
        copy.wait()


def local_pair(
    doc_lengths,
    ssm_x,
    ssm_gate,
    ssm_b,
    ssm_c,
    step_size,
    decay_rate,
    norm_weight,
    queries,
    keys,
    values,
):
    tok, width = ssm_x.shape
    rows, half = 2 * tok, width // 2
    groups = step_size.shape[1] * GROUPS // HEADS // 2
    state = ssm_b.shape[1] // (2 * groups)
    piece = half // groups // PIECES
    kv_half = keys.shape[1] // 2
    q_half = queries.shape[1] // 2
    pieces = groups * PIECES
    copies = 16 + 2 * pieces + 6 * SHARES + 6
    any_spec = pl.BlockSpec(memory_space=pl.ANY)
    vmem_spec = pl.BlockSpec(memory_space=pltpu.VMEM)
    part = rows // 4
    scratch = [
        pltpu.VMEM((rows, half), BF16),
        pltpu.VMEM((rows, half), BF16),
        pltpu.VMEM((rows, groups * state), BF16),
        pltpu.VMEM((rows, groups * state), BF16),
        pltpu.VMEM((step_size.shape[1] // 2, rows), F32),
        pltpu.VMEM((rows, q_half), BF16),
        pltpu.VMEM((3 * rows, kv_half), BF16),
        pltpu.VMEM((3 * rows, kv_half), BF16),
        pltpu.VMEM((pieces, state, piece), BF16),
        pltpu.VMEM((pieces, state, piece), BF16),
        pltpu.VMEM((pieces, state, piece), BF16),
        pltpu.VMEM((8, 128), F32),
        pltpu.VMEM((8, 128), F32),
        pltpu.VMEM((8, 128), F32),
        pltpu.VMEM((rows, half), F32),
        pltpu.VMEM((rows, half), BF16),
        pltpu.VMEM((rows, q_half), BF16),
        pltpu.VMEM((rows, 3 * rows), F32),
        pltpu.VMEM((rows, 128), F32),
        pltpu.VMEM((128, rows), F32),
        pltpu.VMEM((128, rows), F32),
        pltpu.VMEM((rows, 128), F32),
        pltpu.VMEM((rows, 128), F32),
        pltpu.SemaphoreType.DMA((copies,)),
        pltpu.SemaphoreType.DMA((copies,)),
        pltpu.SemaphoreType.DMA((copies,)),
    ]
    mixed, attended = pl.pallas_call(
        functools.partial(pair_kernel, lax.axis_size("ctx")),
        out_shape=(
            jax.ShapeDtypeStruct((part, 4 * half), BF16),
            jax.ShapeDtypeStruct((part, 4 * q_half), BF16),
        ),
        in_specs=[pl.BlockSpec(memory_space=pltpu.SMEM)] + [any_spec] * 8 + [vmem_spec] * 2,
        out_specs=(any_spec, any_spec),
        scratch_shapes=scratch,
        compiler_params=pltpu.CompilerParams(collective_id=0, has_side_effects=True),
    )(
        doc_lengths,
        ssm_x,
        ssm_gate,
        ssm_b,
        ssm_c,
        step_size.T,
        queries,
        keys,
        values,
        decay_rate[None, :],
        norm_weight[None, :],
    )
    return (mixed, attended)


def solution(mesh):
    tp = mesh.shape["tp"]
    paired = tp == 2 and mesh.shape["ctx"] % 4 == 0 and mesh.shape["ctx"] > 4 and GROUPS // tp % 2 == 0
    return jax.shard_map(
        local_pair if paired else local_any,
        mesh=mesh,
        in_specs=(
            P(),
            P("ctx", "tp"),
            P("ctx", "tp"),
            P("ctx", "tp"),
            P("ctx", "tp"),
            P("ctx", "tp"),
            P("tp"),
            P("tp"),
            P("ctx", "tp"),
            P("ctx", "tp"),
            P("ctx", "tp"),
        ),
        out_specs=(P(("ctx", "tp"), None), P(("ctx", "tp"), None)),
        check_vma=False,
    )
```
